32 devices in a mesh: seqa: 2 (over y), seqb: 4 (over z), tp: 4 (over x, core).
Axes of the slice: x: 2, y: 2, z: 4, core: 2. Of those that a mesh axis runs over, the one named last changes fastest.
Arguments:
- queries: bfloat16 [4096, 1024], P(('seqa', 'seqb'), 'tp'), may hold values from -6 to 6
- key_rows: bfloat16 [4096, 1024], P(('seqa', 'seqb'), 'tp'), may hold values from -6 to 6
- value_rows: bfloat16 [4096, 1024], P(('seqa', 'seqb'), 'tp'), may hold values from -6 to 6
- out_grad: bfloat16 [4096, 2048], P(('seqa', 'seqb'), 'tp'), may hold values from -6 to 6
- out_weight: bfloat16 [1024, 2048], P('tp'), may hold values from -0.1875 to 0.1875
- level_codes: int32 [4096, 160], P(('seqa', 'seqb'), 'tp'), may hold values from 0 to 7
Outputs:
- query_grad: bfloat16 [4096, 1024], P(('seqa', 'seqb'), 'tp')
- key_grad: bfloat16 [4096, 1024], P(('seqa', 'seqb'), 'tp')
- value_grad: bfloat16 [4096, 1024], P(('seqa', 'seqb'), 'tp')
The draws below stay inside these ranges and needn't reach their ends.
All inputs are finite; a program needn't handle non-finite values.
Results may differ from the reference program's by a relative error of at most 0.0062.
Values may be sent and summed in bfloat16 or wider, within the bound.
A program may use at most 64 MiB of HBM per device.

```python
import math
import jax
import jax.numpy as jnp
from jax import lax

D = 2048
HEAD_DIM = 128
LEVMAX = 20
TOK_DEV = 512
HEADS = 8
TOKENS = 4096
LEVT = 9
LEVB = 3
N_SEQA = 2
N_SEQB = 4


def plant(drawn, rng, least, largest):
    dims = drawn.shape
    index_at = [jax.random.randint(jax.random.fold_in(rng, axis), (), 0, dims[axis]) for axis in range(len(dims))]
    drawn = drawn.at[tuple(index_at)].set(least)
    longest = dims.index(max(dims))
    index_at[longest] = (index_at[longest] + 1) % dims[longest]
    return drawn.at[tuple(index_at)].set(largest)


def level_of(stream_key, dims, cuts, least, top_value):
    loudness = 1.0
    for axis_at, parts in cuts:
        heights = jax.random.uniform(jax.random.fold_in(jax.random.fold_in(stream_key, 6), axis_at), (parts,), jnp.float32, least / len(cuts), top_value / len(cuts))
        loudness = loudness * jnp.repeat(jnp.exp(heights), dims[axis_at] // parts).reshape((-1,) + (1,) * (len(dims) - 1 - axis_at))
    return loudness


def scatter_about(own_key, dims, deviation, reach, shards=(), kind=jnp.bfloat16):
    entries = jax.random.normal(own_key, dims, jnp.float32) * deviation
    if len(shards) > 0:
        entries = level_of(own_key, dims, shards, -0.22, 0.18) * entries
    return jnp.clip(entries, min=-reach, max=reach).astype(kind)


def setup_inputs(seed: int = 0) -> dict:
    seeds = jax.random.split(jax.random.key(seed), 7)
    return {
        "queries": scatter_about(seeds[0], (TOKENS, HEADS * HEAD_DIM), 1.0, 6.0, ((0, 8), (1, 4))),
        "key_rows": scatter_about(seeds[1], (TOKENS, HEADS * HEAD_DIM), 1.0, 6.0, ((0, 8), (1, 4))),
        "value_rows": scatter_about(seeds[2], (TOKENS, HEADS * HEAD_DIM), 1.0, 6.0, ((0, 8), (1, 4))),
        "out_grad": scatter_about(seeds[3], (TOKENS, D), 1.0, 6.0, ((0, 8), (1, 4))),
        "out_weight": scatter_about(seeds[4], (HEADS * HEAD_DIM, D), (HEADS * HEAD_DIM) ** -0.5, 0.1875, ((0, 4),)),
        "level_codes": plant(jax.random.randint(seeds[5], (TOKENS, HEADS * LEVMAX), 0, 8), jax.random.fold_in(seeds[5], 1), 0, 7).astype(jnp.int32),
    }


def round_trip(value):
    return lax.optimization_barrier(value.astype(jnp.bfloat16)).astype(jnp.float32)

def reference(queries, key_rows, value_rows, out_grad, out_weight, level_codes):
    blocks = N_SEQA * N_SEQB
    head_count = HEADS
    scale_factor = 1.0 / math.sqrt(HEAD_DIM * TOKENS)
    head_grad = jnp.dot(out_grad, out_weight.T, preferred_element_type=jnp.float32).astype(jnp.bfloat16)
    level_weight = ((1 + level_codes).astype(jnp.float32) / 8.0).reshape(blocks, TOK_DEV, head_count, LEVMAX)
    shape_four = (blocks, TOK_DEV, head_count, HEAD_DIM)
    query_full = queries.astype(jnp.float32).reshape(shape_four)
    key_full = key_rows.astype(jnp.float32).reshape(shape_four)
    value_full = value_rows.astype(jnp.float32).reshape(shape_four)
    grad_full = head_grad.astype(jnp.float32).reshape(shape_four)
    position = jnp.arange(TOK_DEV, dtype=jnp.int32)
    differ = jnp.bitwise_xor(position[:, None], position[None, :])
    level_map = jnp.zeros((TOK_DEV, TOK_DEV), jnp.int32)
    for bit_index in range(LEVT):
        level_map = level_map + (differ >= 2 ** bit_index).astype(jnp.int32)
    causal = position[None, :] <= position[:, None]
    one_hot = ((level_map[:, :, None] == jnp.arange(LEVT + 1, dtype=jnp.int32)[None, None, :]) & causal[:, :, None]).astype(jnp.float32)

    def intra(pieces):
        query_blk, key_blk, value_blk, grad_blk, weight_blk = pieces
        weight = jnp.einsum('tsj,thj->hts', one_hot, weight_blk[:, :, :LEVT + 1]) * scale_factor
        scores = jnp.einsum('thk,shk->hts', query_blk, key_blk)
        probs = round_trip(weight * scores)
        dscore = jnp.einsum('thv,shv->hts', grad_blk, value_blk)
        grad_mat = round_trip(weight * dscore)
        query_part = jnp.einsum('hts,shk->thk', grad_mat, key_blk)
        key_portion = jnp.einsum('hts,thk->shk', grad_mat, query_blk)
        value_part = jnp.einsum('hts,thv->shv', probs, grad_blk)
        return (query_part, key_portion, value_part)
    query_intra, key_intra, value_intra = lax.map(intra, (query_full, key_full, value_full, grad_full, level_weight))
    carried_state = jnp.einsum('bthk,bthv->bhkv', key_full, value_full)
    inter_sum = jnp.zeros(shape_four, jnp.float32)
    adjoint = jnp.zeros(carried_state.shape, jnp.float32)
    for bit_index in range(LEVB):
        groups = blocks // 2 ** (bit_index + 1)
        grouping_layout = (groups, 2, 2 ** bit_index, head_count, HEAD_DIM, HEAD_DIM)
        left_sum = carried_state.reshape(grouping_layout)[:, 0].sum(1)
        level_state = jnp.stack([jnp.zeros_like(left_sum), left_sum], 1)[:, :, None]
        level_state = jnp.broadcast_to(level_state, grouping_layout).reshape(carried_state.shape)
        state_bf = round_trip(level_state)
        inter_weight = level_weight[:, :, :, LEVT + 1 + bit_index]
        inter_sum = inter_sum + inter_weight[..., None] * jnp.einsum('bthv,bhkv->bthk', grad_full, state_bf)
        scaled = round_trip(inter_weight[..., None] * grad_full)
        level_adjoint = scale_factor * jnp.einsum('bthk,bthv->bhkv', query_full, scaled)
        right_sum = level_adjoint.reshape(grouping_layout)[:, 1].sum(1)
        spread = jnp.stack([right_sum, jnp.zeros_like(right_sum)], 1)[:, :, None]
        adjoint = adjoint + jnp.broadcast_to(spread, grouping_layout).reshape(carried_state.shape)
    adjoint_bfloat = round_trip(adjoint)
    query_grad = (query_intra + scale_factor * inter_sum).astype(jnp.bfloat16)
    key_grad = (key_intra + jnp.einsum('bthv,bhkv->bthk', value_full, adjoint_bfloat)).astype(jnp.bfloat16)
    value_grad = (value_intra + jnp.einsum('bthk,bhkv->bthv', key_full, adjoint_bfloat)).astype(jnp.bfloat16)
    flat = (TOKENS, head_count * HEAD_DIM)
    return (query_grad.reshape(flat), key_grad.reshape(flat), value_grad.reshape(flat))
```

```python
import functools
import math

import jax
import jax.numpy as jnp
from jax import lax
from jax.experimental import pallas as pl
from jax.experimental.pallas import tpu as pltpu
from jax.sharding import PartitionSpec as P

HEAD_DIM = 128
CHUNK = 128
MESH = pl.DeviceIdType.MESH
F32 = jnp.float32
BF16 = jnp.bfloat16


def dot(a, b, contract):
    return lax.dot_general(a, b, ((contract[:1], contract[1:]), ((), ())), preferred_element_type=F32)


def kernel(
    sizes,
    q_hbm, k_hbm, v_hbm, g_hbm, w_hbm, codes_hbm,
    qg_hbm, kg_hbm, vg_hbm,
    q_ref, k_ref, v_ref, codes_ref, lam_ref, gbuf, wbuf, hg_ref, probs_ref, gm_ref, diag_ref,
    qi_ref, ki_ref, vi_ref, la_ref, psum_ref, psend, precv, asend, arecv, out_ref,
    load_sem, wload_sem, gload_sem, store_sem,
    cross_send, cross_recv, fwd_send, fwd_recv, own_send, own_recv,
    state_send, state_recv, adj_send, adj_recv,
):
    seqa, seqb, tp, rows, heads, feat, scale = sizes
    chips = tp // 2
    chunks = rows // CHUNK
    levels = (seqa * seqb).bit_length() - 1
    top = rows.bit_length() - 1
    levmax = codes_hbm.shape[1] // heads
    ia, ib, it = lax.axis_index("seqa"), lax.axis_index("seqb"), lax.axis_index("tp")
    chip, core = it // 2, it % 2
    block = ia * seqb + ib

    def chip_at(offset):
        return lax.rem(chip + offset + chips, chips)

    partner = (ia, ib, chip * 2 + (1 - core))
    bit, mate = [], []
    for j in range(levels):
        value = (block // 2**j) % 2
        other = block + (1 - 2 * value) * 2**j
        bit.append(value)
        mate.append((other // seqb, other % seqb, it))
    crossing = [(ia, ib, chip_at(-k) * 2 + core) for k in range(chips)]

    barrier = pltpu.get_barrier_semaphore()
    peers = [partner] + crossing[1:] + mate
    for peer in peers:
        pl.semaphore_signal(barrier, inc=1, device_id=peer, device_id_type=MESH)

    loads = [
        pltpu.make_async_copy(src, dst, load_sem.at[i])
        for i, (src, dst) in enumerate(
            [(k_hbm, k_ref), (v_hbm, v_ref), (q_hbm, q_ref), (codes_hbm, codes_ref)]
        )
    ]
    for load in loads:
        load.start()
    gload = pltpu.make_async_copy(g_hbm, gbuf.at[0, 0], gload_sem)
    gload.start()
    wloads = []
    for k in range(chips):
        for cc in range(2):
            src = chip_at(k) * 2 + (core if cc == 0 else 1 - core)
            columns = pl.ds(pl.multiple_of(src * feat, feat), feat)
            copy = pltpu.make_async_copy(w_hbm.at[:, columns], wbuf.at[k, cc], wload_sem.at[k, cc])
            copy.start()
            wloads.append(copy)

    pl.semaphore_wait(barrier, len(peers))

    def rows_of(c):
        return pl.ds(c * CHUNK, CHUNK)

    def remote(src, dst, send, recv, device):
        return pltpu.make_async_remote_copy(
            src_ref=src, dst_ref=dst, send_sem=send, recv_sem=recv, device_id=device, device_id_type=MESH
        )

    cross = {}
    for c in range(chunks):
        for k in range(1, chips):
            cross[k, c] = remote(
                g_hbm.at[rows_of(c)], gbuf.at[k, 0, rows_of(c)],
                cross_send.at[k, c], cross_recv.at[k, c], crossing[k],
            )
            cross[k, c].start()
    own = remote(g_hbm, gbuf.at[0, 1], own_send, own_recv, partner)
    own.start()

    def cols(h):
        return slice(h * HEAD_DIM, (h + 1) * HEAD_DIM)

    loads[0].wait()
    loads[1].wait()
    state_copies = [
        remote(psend.at[j], precv.at[j], state_send.at[j], state_recv.at[j], mate[j]) for j in range(levels)
    ]
    for h in range(heads):
        state = dot(k_ref[:, cols(h)], v_ref[:, cols(h)], (0, 0))
        psum_ref[h] = state
        psend[0, h] = state.astype(BF16)
    state_copies[0].start()

    def state_step(j):
        state_copies[j].wait_recv()
        if j + 1 < levels:
            total = psum_ref[...] + precv[j].astype(F32)
            psum_ref[...] = total
            psend[j + 1] = total.astype(BF16)
            state_copies[j + 1].start()

    loads[2].wait()
    loads[3].wait()
    lam_ref[...] = (1 + codes_ref[...]).astype(F32) / 8.0

    def lam(c, h, level):
        at = h * levmax + level
        return lam_ref[c * CHUNK:(c + 1) * CHUNK, at:at + 1]

    row_at = lax.broadcasted_iota(jnp.int32, (CHUNK, CHUNK), 0)
    col_at = lax.broadcasted_iota(jnp.int32, (CHUNK, CHUNK), 1)
    differ = jnp.bitwise_xor(row_at, col_at)
    inner = CHUNK.bit_length() - 1
    causal = col_at <= row_at
    for h in range(heads):
        for c in range(chunks):
            weight = jnp.broadcast_to(lam(c, h, 0), (CHUNK, CHUNK))
            for level in range(1, inner + 1):
                weight = jnp.where(differ >= 2 ** (level - 1), lam(c, h, level), weight)
            diag_ref[h, c] = jnp.where(causal, weight, 0.0) * scale

    def weighted(c, h, values):
        pieces = []
        for s in range(c):
            factor = lam(c, h, inner + (c ^ s).bit_length()) * scale
            pieces.append((values[:, s * CHUNK:(s + 1) * CHUNK] * factor).astype(BF16))
        pieces.append((values[:, c * CHUNK:] * diag_ref[h, c]).astype(BF16))
        return pieces

    def attend(c, h, target, left_ref, right_ref):
        left = left_ref[c * CHUNK:(c + 1) * CHUNK, cols(h)]
        values = dot(left, right_ref[:(c + 1) * CHUNK, cols(h)], (1, 1))
        for s, piece in enumerate(weighted(c, h, values)):
            target[h, c * CHUNK:(c + 1) * CHUNK, s * CHUNK:(s + 1) * CHUNK] = piece

    for h in range(heads):
        for c in range(chunks):
            attend(c, h, probs_ref, q_ref, k_ref)

    gload.wait()
    for copy in wloads:
        copy.wait()

    def intra_rows(c):
        for h in range(heads):
            attend(c, h, gm_ref, hg_ref, v_ref)
            width = (c + 1) * CHUNK
            qi_ref[c * CHUNK:width, cols(h)] = dot(
                gm_ref[h, c * CHUNK:width, :width], k_ref[:width, cols(h)], (1, 0)
            )

    fwd = {}
    for c in range(chunks):
        here = slice(c * CHUNK, (c + 1) * CHUNK)
        partial = dot(gbuf[0, 0, here], wbuf[0, 0], (1, 1))
        if c == 0:
            own.wait_recv()
        partial = partial + dot(gbuf[0, 1, here], wbuf[0, 1], (1, 1))
        for k in range(1, chips):
            cross[k, c].wait_recv()
            fwd[k, c] = remote(
                gbuf.at[k, 0, rows_of(c)], gbuf.at[k, 1, rows_of(c)],
                fwd_send.at[k, c], fwd_recv.at[k, c], partner,
            )
            fwd[k, c].start()
            partial = partial + dot(gbuf[k, 0, here], wbuf[k, 0], (1, 1))
        for k in range(1, chips):
            fwd[k, c].wait_recv()
            partial = partial + dot(gbuf[k, 1, here], wbuf[k, 1], (1, 1))
        head_grad = partial.astype(BF16)
        hg_ref[here] = head_grad
        wide = head_grad.astype(F32)
        for h in range(heads):
            for i in range(levels):
                scaled = (lam(c, h, top + 1 + i) * wide[:, cols(h)]).astype(BF16)
                part = dot(q_ref[here, cols(h)], scaled, (0, 0)) * scale
                la_ref[i, h] = part if c == 0 else la_ref[i, h] + part
        if c < chunks - 1:
            intra_rows(c)
            if c < levels:
                state_step(c)

    adj = {
        (j, h): remote(asend.at[j, h], arecv.at[j, h], adj_send.at[j, h], adj_recv.at[j, h], mate[j])
        for j in range(levels)
        for h in range(heads)
    }
    for h in range(heads):
        asend[levels - 1, h] = jnp.where(bit[levels - 1] == 1, la_ref[levels - 1, h], 0.0).astype(BF16)
        adj[levels - 1, h].start()

    def tail_rows():
        intra_rows(chunks - 1)

    def tail_inter():
        for j in range(chunks - 1, levels):
            state_step(j)
        for h in range(heads):
            for c in range(chunks):
                here = slice(c * CHUNK, (c + 1) * CHUNK)
                total = jnp.zeros((CHUNK, HEAD_DIM), F32)
                for i in range(levels):
                    kept = jnp.where(bit[i] == 1, precv[i, h].astype(F32), 0.0).astype(BF16)
                    total = total + lam(c, h, top + 1 + i) * dot(hg_ref[here, cols(h)], kept, (1, 1))
                out_ref[0, here, cols(h)] = (qi_ref[here, cols(h)] + scale * total).astype(BF16)
        stores[0].start()

    def tail_columns():
        for h in range(heads):
            for s in range(chunks):
                start = s * CHUNK
                at = slice(start, start + CHUNK)
                ki_ref[at, cols(h)] = dot(gm_ref[h, start:, at], q_ref[start:, cols(h)], (0, 0))
                vi_ref[at, cols(h)] = dot(probs_ref[h, start:, at], hg_ref[start:, cols(h)], (0, 0))

    stores = [
        pltpu.make_async_copy(out_ref.at[i], ref, store_sem.at[i]) for i, ref in enumerate((qg_hbm, kg_hbm, vg_hbm))
    ]
    work = [tail_rows, tail_inter, tail_columns]
    total = [jnp.zeros((HEAD_DIM, HEAD_DIM), F32)] * heads
    for j in range(levels - 1, -1, -1):
        if work:
            work.pop(0)()
        for h in range(heads):
            adj[j, h].wait_recv()
            total[h] = total[h] + arecv[j, h].astype(F32)
            if j > 0:
                asend[j - 1, h] = (total[h] + jnp.where(bit[j - 1] == 1, la_ref[j - 1, h], 0.0)).astype(BF16)
                adj[j - 1, h].start()
    for piece in work:
        piece()
    for h in range(heads):
        adjoint = total[h].astype(BF16)
        out_ref[1, :, cols(h)] = (ki_ref[:, cols(h)] + dot(v_ref[:, cols(h)], adjoint, (1, 1))).astype(BF16)
        out_ref[2, :, cols(h)] = (vi_ref[:, cols(h)] + dot(k_ref[:, cols(h)], adjoint, (1, 0))).astype(BF16)
    stores[1].start()
    stores[2].start()
    for copy in cross.values():
        copy.wait_send()
    for copy in fwd.values():
        copy.wait_send()
    own.wait_send()
    for copy in state_copies:
        copy.wait_send()
    for copy in adj.values():
        copy.wait_send()
    for store in stores:
        store.wait()


def solution(mesh):
    seqa, seqb, tp = (mesh.shape[name] for name in ("seqa", "seqb", "tp"))
    levels = (seqa * seqb).bit_length() - 1

    def per_device(queries, key_rows, value_rows, out_grad, out_weight, level_codes):
        rows, width = queries.shape
        heads = width // HEAD_DIM
        feat = out_grad.shape[1]
        chips = tp // 2
        chunks = rows // CHUNK
        scale = 1.0 / math.sqrt(HEAD_DIM * rows * seqa * seqb)
        square = (HEAD_DIM, HEAD_DIM)
        dma = pltpu.SemaphoreType.DMA
        result = jax.ShapeDtypeStruct((rows, width), BF16)
        return pl.pallas_call(
            functools.partial(kernel, (seqa, seqb, tp, rows, heads, feat, scale)),
            out_shape=(result,) * 3,
            in_specs=[pl.BlockSpec(memory_space=pl.ANY)] * 6,
            out_specs=(pl.BlockSpec(memory_space=pl.ANY),) * 3,
            scratch_shapes=[
                pltpu.VMEM((rows, width), BF16),
                pltpu.VMEM((rows, width), BF16),
                pltpu.VMEM((rows, width), BF16),
                pltpu.VMEM(level_codes.shape, jnp.int32),
                pltpu.VMEM(level_codes.shape, F32),
                pltpu.VMEM((chips, 2, rows, feat), BF16),
                pltpu.VMEM((chips, 2, width, feat), BF16),
                pltpu.VMEM((rows, width), BF16),
                pltpu.VMEM((heads, rows, rows), BF16),
                pltpu.VMEM((heads, rows, rows), BF16),
                pltpu.VMEM((heads, chunks, CHUNK, CHUNK), F32),
                pltpu.VMEM((rows, width), F32),
                pltpu.VMEM((rows, width), F32),
                pltpu.VMEM((rows, width), F32),
                pltpu.VMEM((levels, heads) + square, F32),
                pltpu.VMEM((heads,) + square, F32),
                pltpu.VMEM((levels, heads) + square, BF16),
                pltpu.VMEM((levels, heads) + square, BF16),
                pltpu.VMEM((levels, heads) + square, BF16),
                pltpu.VMEM((levels, heads) + square, BF16),
                pltpu.VMEM((3, rows, width), BF16),
                dma((4,)),
                dma((chips, 2)),
                dma,
                dma((3,)),
                dma((chips, chunks)),
                dma((chips, chunks)),
                dma((chips, chunks)),
                dma((chips, chunks)),
                dma,
                dma,
                dma((levels,)),
                dma((levels,)),
                dma((levels, heads)),
                dma((levels, heads)),
            ],
            compiler_params=pltpu.CompilerParams(
                collective_id=0, has_side_effects=True, vmem_limit_bytes=40 * 1024 * 1024
            ),
        )(queries, key_rows, value_rows, out_grad, out_weight, level_codes)

    sharded = P(("seqa", "seqb"), "tp")
    return jax.shard_map(
        per_device,
        mesh=mesh,
        in_specs=(sharded,) * 4 + (P("tp", None), sharded),
        out_specs=(sharded,) * 3,
        check_vma=False,
    )
```

```python
import functools
import math

import jax
import jax.numpy as jnp
from jax import lax
from jax.experimental import pallas as pl
from jax.experimental.pallas import tpu as pltpu
from jax.sharding import PartitionSpec as P

HEAD_DIM = 128
CHUNK = 128
PIECES = 2
MESH = pl.DeviceIdType.MESH
F32 = jnp.float32
BF16 = jnp.bfloat16


def dot(a, b, contract):
    return lax.dot_general(a, b, ((contract[:1], contract[1:]), ((), ())), preferred_element_type=F32)


def kernel(
    sizes,
    q_hbm, k_hbm, v_hbm, g_hbm, w_hbm, codes_hbm,
    qg_ref, kg_ref, vg_ref,
    q_ref, k_ref, v_ref, codes_ref, lam_ref, gbuf, wbuf, hg_ref, probs_ref, gm_ref, diag_ref,
    qi_ref, ki_ref, vi_ref, la_ref, psum_ref, asum_ref, psend, precv, asend, arecv,
    load_sem, wload_sem, gload_sem,
    cross_send, cross_recv, fwd_send, fwd_recv, own_send, own_recv,
    state_send, state_recv, adj_send, adj_recv,
):
    seqa, seqb, tp, rows, heads, feat, scale = sizes
    chips = tp // 2
    chunks = rows // CHUNK
    levels = (seqa * seqb).bit_length() - 1
    top = rows.bit_length() - 1
    levmax = codes_hbm.shape[0] // heads
    ia, ib, it = lax.axis_index("seqa"), lax.axis_index("seqb"), lax.axis_index("tp")
    chip, core = it // 2, it % 2
    block = ia * seqb + ib

    def chip_at(offset):
        return lax.rem(chip + offset + chips, chips)

    partner = (ia, ib, chip * 2 + (1 - core))
    bit, mate = [], []
    for j in range(levels):
        value = (block // 2**j) % 2
        other = block + (1 - 2 * value) * 2**j
        bit.append(value)
        mate.append((other // seqb, other % seqb, it))
    crossing = [(ia, ib, chip_at(-k) * 2 + core) for k in range(chips)]

    barrier = pltpu.get_barrier_semaphore()
    peers = [partner] + crossing[1:] + mate
    for peer in peers:
        pl.semaphore_signal(barrier, inc=1, device_id=peer, device_id_type=MESH)

    loads = [
        pltpu.make_async_copy(src, dst, load_sem.at[i])
        for i, (src, dst) in enumerate(
            [(k_hbm, k_ref), (v_hbm, v_ref), (q_hbm, q_ref), (codes_hbm, codes_ref)]
        )
    ]
    for load in loads:
        load.start()
    gload = pltpu.make_async_copy(g_hbm, gbuf.at[0, 0], gload_sem)
    gload.start()
    wloads = []
    for k in range(chips):
        for cc in range(2):
            src = chip_at(k) * 2 + (core if cc == 0 else 1 - core)
            columns = pl.ds(pl.multiple_of(src * feat, feat), feat)
            copy = pltpu.make_async_copy(w_hbm.at[:, columns], wbuf.at[k, cc], wload_sem.at[k, cc])
            copy.start()
            wloads.append(copy)

    pl.semaphore_wait(barrier, len(peers))

    def rows_of(c):
        return pl.ds(c * CHUNK, CHUNK)

    def remote(src, dst, send, recv, device):
        return pltpu.make_async_remote_copy(
            src_ref=src, dst_ref=dst, send_sem=send, recv_sem=recv, device_id=device, device_id_type=MESH
        )

    cross = {}
    for c in range(chunks):
        for k in range(1, chips):
            cross[k, c] = remote(
                g_hbm.at[rows_of(c)], gbuf.at[k, 0, rows_of(c)],
                cross_send.at[k, c], cross_recv.at[k, c], crossing[k],
            )
            cross[k, c].start()
    own = remote(g_hbm, gbuf.at[0, 1], own_send, own_recv, partner)
    own.start()

    def cols(h):
        return slice(h * HEAD_DIM, (h + 1) * HEAD_DIM)

    loads[0].wait()
    loads[1].wait()
    state_copies = [
        remote(psend.at[j], precv.at[j], state_send.at[j], state_recv.at[j], mate[j]) for j in range(levels)
    ]
    for h in range(heads):
        state = dot(k_ref[:, cols(h)], v_ref[:, cols(h)], (0, 0))
        psum_ref[h] = state
        psend[0, h] = state.astype(BF16)
    state_copies[0].start()

    def state_step(j):
        state_copies[j].wait_recv()
        if j + 1 < levels:
            total = psum_ref[...] + precv[j].astype(F32)
            psum_ref[...] = total
            psend[j + 1] = total.astype(BF16)
            state_copies[j + 1].start()

    loads[2].wait()
    loads[3].wait()
    lam_ref[...] = ((1 + codes_ref[...]).astype(F32) / 8.0).T

    def lam(c, h, level):
        at = h * levmax + level
        return lam_ref[c * CHUNK:(c + 1) * CHUNK, at:at + 1]

    row_at = lax.broadcasted_iota(jnp.int32, (CHUNK, CHUNK), 0)
    col_at = lax.broadcasted_iota(jnp.int32, (CHUNK, CHUNK), 1)
    differ = jnp.bitwise_xor(row_at, col_at)
    inner = CHUNK.bit_length() - 1
    causal = col_at <= row_at
    for h in range(heads):
        for c in range(chunks):
            weight = jnp.broadcast_to(lam(c, h, 0), (CHUNK, CHUNK))
            for level in range(1, inner + 1):
                weight = jnp.where(differ >= 2 ** (level - 1), lam(c, h, level), weight)
            diag_ref[h, c] = jnp.where(causal, weight, 0.0) * scale

    def weighted(c, h, values):
        pieces = []
        for s in range(c):
            factor = lam(c, h, inner + (c ^ s).bit_length()) * scale
            pieces.append((values[:, s * CHUNK:(s + 1) * CHUNK] * factor).astype(BF16))
        pieces.append((values[:, c * CHUNK:] * diag_ref[h, c]).astype(BF16))
        return pieces

    def attend(c, h, target, left_ref, right_ref):
        left = left_ref[c * CHUNK:(c + 1) * CHUNK, cols(h)]
        values = dot(left, right_ref[:(c + 1) * CHUNK, cols(h)], (1, 1))
        for s, piece in enumerate(weighted(c, h, values)):
            target[h, c * CHUNK:(c + 1) * CHUNK, s * CHUNK:(s + 1) * CHUNK] = piece

    for h in range(heads):
        for c in range(chunks):
            attend(c, h, probs_ref, q_ref, k_ref)

    gload.wait()
    for copy in wloads:
        copy.wait()

    def intra_rows(c):
        for h in range(heads):
            attend(c, h, gm_ref, hg_ref, v_ref)
            width = (c + 1) * CHUNK
            qi_ref[c * CHUNK:width, cols(h)] = dot(
                gm_ref[h, c * CHUNK:width, :width], k_ref[:width, cols(h)], (1, 0)
            )

    step_rows = HEAD_DIM // PIECES
    adj = {}
    for j in range(levels):
        for h in range(heads):
            for p in range(PIECES):
                at = pl.ds(p * step_rows, step_rows)
                adj[j, h, p] = remote(
                    asend.at[j, h, at], arecv.at[j, h, at],
                    adj_send.at[j, h, p], adj_recv.at[j, h, p], mate[j],
                )

    def send_adjoint(j, h, value):
        for p in range(PIECES):
            at = slice(p * step_rows, (p + 1) * step_rows)
            asend[j, h, at] = value[at].astype(BF16)
            adj[j, h, p].start()

    fwd = {}
    for c in range(chunks):
        here = slice(c * CHUNK, (c + 1) * CHUNK)
        partial = dot(gbuf[0, 0, here], wbuf[0, 0], (1, 1))
        if c == 0:
            own.wait_recv()
        partial = partial + dot(gbuf[0, 1, here], wbuf[0, 1], (1, 1))
        for k in range(1, chips):
            cross[k, c].wait_recv()
            fwd[k, c] = remote(
                gbuf.at[k, 0, rows_of(c)], gbuf.at[k, 1, rows_of(c)],
                fwd_send.at[k, c], fwd_recv.at[k, c], partner,
            )
            fwd[k, c].start()
            partial = partial + dot(gbuf[k, 0, here], wbuf[k, 0], (1, 1))
        for k in range(1, chips):
            fwd[k, c].wait_recv()
            partial = partial + dot(gbuf[k, 1, here], wbuf[k, 1], (1, 1))
        head_grad = partial.astype(BF16)
        hg_ref[here] = head_grad
        wide = head_grad.astype(F32)
        for i in range(levels - 1, -1, -1):
            for h in range(heads):
                scaled = (lam(c, h, top + 1 + i) * wide[:, cols(h)]).astype(BF16)
                part = dot(q_ref[here, cols(h)], scaled, (0, 0)) * scale
                part = part if c == 0 else la_ref[i, h] + part
                la_ref[i, h] = part
                if c == chunks - 1 and i == levels - 1:
                    send_adjoint(i, h, jnp.where(bit[i] == 1, part, 0.0))
        if c < chunks - 1:
            intra_rows(c)
            if c < levels:
                state_step(c)

    def tail_rows():
        intra_rows(chunks - 1)

    def tail_inter():
        for j in range(chunks - 1, levels):
            state_step(j)
        for h in range(heads):
            for c in range(chunks):
                here = slice(c * CHUNK, (c + 1) * CHUNK)
                total = jnp.zeros((CHUNK, HEAD_DIM), F32)
                for i in range(levels):
                    kept = jnp.where(bit[i] == 1, precv[i, h].astype(F32), 0.0).astype(BF16)
                    total = total + lam(c, h, top + 1 + i) * dot(hg_ref[here, cols(h)], kept, (1, 1))
                qg_ref[here, cols(h)] = (qi_ref[here, cols(h)] + scale * total).astype(BF16)

    def tail_columns():
        for h in range(heads):
            for s in range(chunks):
                start = s * CHUNK
                at = slice(start, start + CHUNK)
                ki_ref[at, cols(h)] = dot(gm_ref[h, start:, at], q_ref[start:, cols(h)], (0, 0))
                vi_ref[at, cols(h)] = dot(probs_ref[h, start:, at], hg_ref[start:, cols(h)], (0, 0))

    work = [tail_rows, tail_inter, tail_columns]
    for j in range(levels - 1, -1, -1):
        if work:
            work.pop(0)()
        for h in range(heads):
            for p in range(PIECES):
                at = slice(p * step_rows, (p + 1) * step_rows)
                adj[j, h, p].wait_recv()
                total = arecv[j, h, at].astype(F32)
                if j < levels - 1:
                    total = asum_ref[h, at] + total
                asum_ref[h, at] = total
                if j > 0:
                    addend = jnp.where(bit[j - 1] == 1, la_ref[j - 1, h, at], 0.0)
                    asend[j - 1, h, at] = (total + addend).astype(BF16)
                    adj[j - 1, h, p].start()
    for piece in work:
        piece()
    for h in range(heads):
        adjoint = asum_ref[h].astype(BF16)
        kg_ref[:, cols(h)] = (ki_ref[:, cols(h)] + dot(v_ref[:, cols(h)], adjoint, (1, 1))).astype(BF16)
        vg_ref[:, cols(h)] = (vi_ref[:, cols(h)] + dot(k_ref[:, cols(h)], adjoint, (1, 0))).astype(BF16)
    for copy in cross.values():
        copy.wait_send()
    for copy in fwd.values():
        copy.wait_send()
    own.wait_send()
    for copy in state_copies:
        copy.wait_send()
    for copy in adj.values():
        copy.wait_send()


def place(*refs):
    sems = refs[6]
    copies = [pltpu.make_async_copy(refs[i], refs[3 + i], sems.at[i]) for i in range(3)]
    for copy in copies:
        copy.start()
    for copy in copies:
        copy.wait()


def solution(mesh):
    seqa, seqb, tp = (mesh.shape[name] for name in ("seqa", "seqb", "tp"))
    levels = (seqa * seqb).bit_length() - 1

    def per_device(queries, key_rows, value_rows, out_grad, out_weight, level_codes):
        rows, width = queries.shape
        heads = width // HEAD_DIM
        feat = out_grad.shape[1]
        chips = tp // 2
        chunks = rows // CHUNK
        scale = 1.0 / math.sqrt(HEAD_DIM * rows * seqa * seqb)
        square = (HEAD_DIM, HEAD_DIM)
        dma = pltpu.SemaphoreType.DMA
        result = jax.ShapeDtypeStruct((rows, width), BF16)
        grads = pl.pallas_call(
            functools.partial(kernel, (seqa, seqb, tp, rows, heads, feat, scale)),
            out_shape=(result,) * 3,
            in_specs=[pl.BlockSpec(memory_space=pltpu.HBM)] * 6,
            out_specs=(pl.BlockSpec(memory_space=pltpu.VMEM),) * 3,
            scratch_shapes=[
                pltpu.VMEM((rows, width), BF16),
                pltpu.VMEM((rows, width), BF16),
                pltpu.VMEM((rows, width), BF16),
                pltpu.VMEM(level_codes.shape[::-1], jnp.int32),
                pltpu.VMEM(level_codes.shape, F32),
                pltpu.VMEM((chips, 2, rows, feat), BF16),
                pltpu.VMEM((chips, 2, width, feat), BF16),
                pltpu.VMEM((rows, width), BF16),
                pltpu.VMEM((heads, rows, rows), BF16),
                pltpu.VMEM((heads, rows, rows), BF16),
                pltpu.VMEM((heads, chunks, CHUNK, CHUNK), F32),
                pltpu.VMEM((rows, width), F32),
                pltpu.VMEM((rows, width), F32),
                pltpu.VMEM((rows, width), F32),
                pltpu.VMEM((levels, heads) + square, F32),
                pltpu.VMEM((heads,) + square, F32),
                pltpu.VMEM((heads,) + square, F32),
                pltpu.VMEM((levels, heads) + square, BF16),
                pltpu.VMEM((levels, heads) + square, BF16),
                pltpu.VMEM((levels, heads) + square, BF16),
                pltpu.VMEM((levels, heads) + square, BF16),
                dma((4,)),
                dma((chips, 2)),
                dma,
                dma((chips, chunks)),
                dma((chips, chunks)),
                dma((chips, chunks)),
                dma((chips, chunks)),
                dma,
                dma,
                dma((levels,)),
                dma((levels,)),
                dma((levels, heads, PIECES)),
                dma((levels, heads, PIECES)),
            ],
            compiler_params=pltpu.CompilerParams(
                collective_id=0, has_side_effects=True, vmem_limit_bytes=32768 * 1024
            ),
        )(*[pltpu.with_memory_space_constraint(x, pltpu.HBM) for x in (queries, key_rows, value_rows, out_grad, out_weight, level_codes.T)])
        return pl.pallas_call(
            place,
            out_shape=(result,) * 3,
            in_specs=[pl.BlockSpec(memory_space=pltpu.VMEM)] * 3,
            out_specs=(pl.BlockSpec(memory_space=pl.ANY),) * 3,
            scratch_shapes=[dma((3,))],
            compiler_params=pltpu.CompilerParams(vmem_limit_bytes=8 * 1024 * 1024),
        )(*grads)

    sharded = P(("seqa", "seqb"), "tp")
    return jax.shard_map(
        per_device,
        mesh=mesh,
        in_specs=(sharded,) * 4 + (P("tp", None), sharded),
        out_specs=(sharded,) * 3,
        check_vma=False,
    )
```

```python
import functools
import math

import jax
import jax.numpy as jnp
from jax import lax
from jax.experimental import pallas as pl
from jax.experimental.pallas import tpu as pltpu
from jax.sharding import PartitionSpec as P

HEAD_DIM = 128
CHUNK = 128
PIECES = 2
MESH = pl.DeviceIdType.MESH
F32 = jnp.float32
BF16 = jnp.bfloat16


def dot(a, b, contract):
    return lax.dot_general(a, b, ((contract[:1], contract[1:]), ((), ())), preferred_element_type=F32)


def kernel(
    sizes,
    q_hbm, k_hbm, v_hbm, g_hbm, w_hbm, codes_hbm,
    qg_ref, kg_ref, vg_ref,
    q_ref, k_ref, v_ref, codes_ref, lam_ref, gbuf, wbuf, hg_ref, probs_ref, gm_ref, diag_ref,
    qi_ref, ki_ref, vi_ref, la_ref, psum_ref, asum_ref, psend, precv, asend, arecv,
    load_sem, wload_sem, gload_sem,
    cross_send, cross_recv, fwd_send, fwd_recv, own_send, own_recv,
    state_send, state_recv, adj_send, adj_recv,
):
    seqa, seqb, tp, rows, heads, feat, scale = sizes
    chips = tp // 2
    chunks = rows // CHUNK
    levels = (seqa * seqb).bit_length() - 1
    top = rows.bit_length() - 1
    levmax = codes_hbm.shape[0] // heads
    ia, ib, it = lax.axis_index("seqa"), lax.axis_index("seqb"), lax.axis_index("tp")
    chip, core = it // 2, it % 2
    block = ia * seqb + ib

    def chip_at(offset):
        return lax.rem(chip + offset + chips, chips)

    partner = (ia, ib, chip * 2 + (1 - core))
    bit, mate = [], []
    for j in range(levels):
        value = (block // 2**j) % 2
        other = block + (1 - 2 * value) * 2**j
        bit.append(value)
        mate.append((other // seqb, other % seqb, it))
    crossing = [(ia, ib, chip_at(-k) * 2 + core) for k in range(chips)]

    barrier = pltpu.get_barrier_semaphore()
    peers = [partner] + crossing[1:] + mate
    for peer in peers:
        pl.semaphore_signal(barrier, inc=1, device_id=peer, device_id_type=MESH)

    loads = [
        pltpu.make_async_copy(src, dst, load_sem.at[i])
        for i, (src, dst) in enumerate(
            [(k_hbm, k_ref), (v_hbm, v_ref), (q_hbm, q_ref), (codes_hbm, codes_ref)]
        )
    ]
    for load in loads:
        load.start()
    gload = pltpu.make_async_copy(g_hbm, gbuf.at[0, 0], gload_sem)
    gload.start()
    wloads = []
    for k in range(chips):
        for cc in range(2):
            src = chip_at(k) * 2 + (core if cc == 0 else 1 - core)
            columns = pl.ds(pl.multiple_of(src * feat, feat), feat)
            copy = pltpu.make_async_copy(w_hbm.at[:, columns], wbuf.at[k, cc], wload_sem.at[k, cc])
            copy.start()
            wloads.append(copy)

    pl.semaphore_wait(barrier, len(peers))

    def rows_of(c):
        return pl.ds(c * CHUNK, CHUNK)

    def remote(src, dst, send, recv, device):
        return pltpu.make_async_remote_copy(
            src_ref=src, dst_ref=dst, send_sem=send, recv_sem=recv, device_id=device, device_id_type=MESH
        )

    cross = {}
    for c in range(chunks):
        for k in range(1, chips):
            cross[k, c] = remote(
                g_hbm.at[rows_of(c)], gbuf.at[k, 0, rows_of(c)],
                cross_send.at[k, c], cross_recv.at[k, c], crossing[k],
            )
            cross[k, c].start()
    own = remote(g_hbm, gbuf.at[0, 1], own_send, own_recv, partner)
    own.start()

    def cols(h):
        return slice(h * HEAD_DIM, (h + 1) * HEAD_DIM)

    loads[0].wait()
    loads[1].wait()
    state_copies = [
        remote(psend.at[j], precv.at[j], state_send.at[j], state_recv.at[j], mate[j]) for j in range(levels)
    ]
    for h in range(heads):
        state = dot(k_ref[:, cols(h)], v_ref[:, cols(h)], (0, 0))
        psum_ref[h] = state
        psend[0, h] = state.astype(BF16)
    state_copies[0].start()

    def state_step(j):
        state_copies[j].wait_recv()
        if j + 1 < levels:
            total = psum_ref[...] + precv[j].astype(F32)
            psum_ref[...] = total
            psend[j + 1] = total.astype(BF16)
            state_copies[j + 1].start()

    loads[2].wait()
    loads[3].wait()
    lam_ref[...] = ((1 + codes_ref[...]).astype(F32) / 8.0).T

    def lam(c, h, level):
        at = h * levmax + level
        return lam_ref[c * CHUNK:(c + 1) * CHUNK, at:at + 1]

    row_at = lax.broadcasted_iota(jnp.int32, (CHUNK, CHUNK), 0)
    col_at = lax.broadcasted_iota(jnp.int32, (CHUNK, CHUNK), 1)
    differ = jnp.bitwise_xor(row_at, col_at)
    inner = CHUNK.bit_length() - 1
    causal = col_at <= row_at
    for h in range(heads):
        for c in range(chunks):
            weight = jnp.broadcast_to(lam(c, h, 0), (CHUNK, CHUNK))
            for level in range(1, inner + 1):
                weight = jnp.where(differ >= 2 ** (level - 1), lam(c, h, level), weight)
            diag_ref[h, c] = jnp.where(causal, weight, 0.0) * scale

    def weighted(c, h, values):
        pieces = []
        for s in range(c):
            factor = lam(c, h, inner + (c ^ s).bit_length()) * scale
            pieces.append((values[:, s * CHUNK:(s + 1) * CHUNK] * factor).astype(BF16))
        pieces.append((values[:, c * CHUNK:] * diag_ref[h, c]).astype(BF16))
        return pieces

    def attend(c, h, target, left_ref, right_ref):
        left = left_ref[c * CHUNK:(c + 1) * CHUNK, cols(h)]
        values = dot(left, right_ref[:(c + 1) * CHUNK, cols(h)], (1, 1))
        for s, piece in enumerate(weighted(c, h, values)):
            target[h, c * CHUNK:(c + 1) * CHUNK, s * CHUNK:(s + 1) * CHUNK] = piece

    for h in range(heads):
        for c in range(chunks):
            attend(c, h, probs_ref, q_ref, k_ref)

    gload.wait()
    for copy in wloads:
        copy.wait()

    def intra_rows(c):
        for h in range(heads):
            attend(c, h, gm_ref, hg_ref, v_ref)
            width = (c + 1) * CHUNK
            qi_ref[c * CHUNK:width, cols(h)] = dot(
                gm_ref[h, c * CHUNK:width, :width], k_ref[:width, cols(h)], (1, 0)
            )

    step_rows = HEAD_DIM // PIECES
    adj = {}
    for j in range(levels):
        for h in range(heads):
            for p in range(PIECES):
                at = pl.ds(p * step_rows, step_rows)
                adj[j, h, p] = remote(
                    asend.at[j, h, at], arecv.at[j, h, at],
                    adj_send.at[j, h, p], adj_recv.at[j, h, p], mate[j],
                )

    def send_adjoint(j, h, value):
        for p in range(PIECES):
            at = slice(p * step_rows, (p + 1) * step_rows)
            asend[j, h, at] = value[at].astype(BF16)
            adj[j, h, p].start()

    state_step(0)
    fwd = {}
    for c in range(chunks):
        here = slice(c * CHUNK, (c + 1) * CHUNK)
        partial = dot(gbuf[0, 0, here], wbuf[0, 0], (1, 1))
        if c == 0:
            own.wait_recv()
        partial = partial + dot(gbuf[0, 1, here], wbuf[0, 1], (1, 1))
        for k in range(1, chips):
            cross[k, c].wait_recv()
            fwd[k, c] = remote(
                gbuf.at[k, 0, rows_of(c)], gbuf.at[k, 1, rows_of(c)],
                fwd_send.at[k, c], fwd_recv.at[k, c], partner,
            )
            fwd[k, c].start()
            partial = partial + dot(gbuf[k, 0, here], wbuf[k, 0], (1, 1))
        for k in range(1, chips):
            fwd[k, c].wait_recv()
            partial = partial + dot(gbuf[k, 1, here], wbuf[k, 1], (1, 1))
        head_grad = partial.astype(BF16)
        hg_ref[here] = head_grad
        wide = head_grad.astype(F32)
        for i in range(levels - 1, -1, -1):
            for h in range(heads):
                scaled = (lam(c, h, top + 1 + i) * wide[:, cols(h)]).astype(BF16)
                part = dot(q_ref[here, cols(h)], scaled, (0, 0)) * scale
                part = part if c == 0 else la_ref[i, h] + part
                la_ref[i, h] = part
                if c == chunks - 1 and i == levels - 1:
                    send_adjoint(i, h, jnp.where(bit[i] == 1, part, 0.0))
        if c < chunks - 1:
            intra_rows(c)
            if c + 1 < levels:
                state_step(c + 1)

    def tail_rows():
        intra_rows(chunks - 1)

    def tail_inter():
        for j in range(chunks, levels):
            state_step(j)
        for h in range(heads):
            for c in range(chunks):
                here = slice(c * CHUNK, (c + 1) * CHUNK)
                total = jnp.zeros((CHUNK, HEAD_DIM), F32)
                for i in range(levels):
                    kept = jnp.where(bit[i] == 1, precv[i, h].astype(F32), 0.0).astype(BF16)
                    total = total + lam(c, h, top + 1 + i) * dot(hg_ref[here, cols(h)], kept, (1, 1))
                qg_ref[here, cols(h)] = (qi_ref[here, cols(h)] + scale * total).astype(BF16)

    def tail_columns():
        for h in range(heads):
            for s in range(chunks):
                start = s * CHUNK
                at = slice(start, start + CHUNK)
                ki_ref[at, cols(h)] = dot(gm_ref[h, start:, at], q_ref[start:, cols(h)], (0, 0))
                vi_ref[at, cols(h)] = dot(probs_ref[h, start:, at], hg_ref[start:, cols(h)], (0, 0))

    work = [tail_rows, tail_inter, tail_columns]
    for j in range(levels - 1, -1, -1):
        if work:
            work.pop(0)()
        for h in range(heads):
            for p in range(PIECES):
                at = slice(p * step_rows, (p + 1) * step_rows)
                adj[j, h, p].wait_recv()
                total = arecv[j, h, at].astype(F32)
                if j < levels - 1:
                    total = asum_ref[h, at] + total
                asum_ref[h, at] = total
                if j > 0:
                    addend = jnp.where(bit[j - 1] == 1, la_ref[j - 1, h, at], 0.0)
                    asend[j - 1, h, at] = (total + addend).astype(BF16)
                    adj[j - 1, h, p].start()
    for piece in work:
        piece()
    for h in range(heads):
        adjoint = asum_ref[h].astype(BF16)
        kg_ref[:, cols(h)] = (ki_ref[:, cols(h)] + dot(v_ref[:, cols(h)], adjoint, (1, 1))).astype(BF16)
        vg_ref[:, cols(h)] = (vi_ref[:, cols(h)] + dot(k_ref[:, cols(h)], adjoint, (1, 0))).astype(BF16)
    for copy in cross.values():
        copy.wait_send()
    for copy in fwd.values():
        copy.wait_send()
    own.wait_send()
    for copy in state_copies:
        copy.wait_send()
    for copy in adj.values():
        copy.wait_send()


def place(*refs):
    sems = refs[6]
    copies = [pltpu.make_async_copy(refs[i], refs[3 + i], sems.at[i]) for i in range(3)]
    for copy in copies:
        copy.start()
    for copy in copies:
        copy.wait()


def solution(mesh):
    seqa, seqb, tp = (mesh.shape[name] for name in ("seqa", "seqb", "tp"))
    levels = (seqa * seqb).bit_length() - 1

    def per_device(queries, key_rows, value_rows, out_grad, out_weight, level_codes):
        rows, width = queries.shape
        heads = width // HEAD_DIM
        feat = out_grad.shape[1]
        chips = tp // 2
        chunks = rows // CHUNK
        scale = 1.0 / math.sqrt(HEAD_DIM * rows * seqa * seqb)
        square = (HEAD_DIM, HEAD_DIM)
        dma = pltpu.SemaphoreType.DMA
        result = jax.ShapeDtypeStruct((rows, width), BF16)
        grads = pl.pallas_call(
            functools.partial(kernel, (seqa, seqb, tp, rows, heads, feat, scale)),
            out_shape=(result,) * 3,
            in_specs=[pl.BlockSpec(memory_space=pltpu.HBM)] * 6,
            out_specs=(pl.BlockSpec(memory_space=pltpu.VMEM),) * 3,
            scratch_shapes=[
                pltpu.VMEM((rows, width), BF16),
                pltpu.VMEM((rows, width), BF16),
                pltpu.VMEM((rows, width), BF16),
                pltpu.VMEM(level_codes.shape[::-1], jnp.int32),
                pltpu.VMEM(level_codes.shape, F32),
                pltpu.VMEM((chips, 2, rows, feat), BF16),
                pltpu.VMEM((chips, 2, width, feat), BF16),
                pltpu.VMEM((rows, width), BF16),
                pltpu.VMEM((heads, rows, rows), BF16),
                pltpu.VMEM((heads, rows, rows), BF16),
                pltpu.VMEM((heads, chunks, CHUNK, CHUNK), F32),
                pltpu.VMEM((rows, width), F32),
                pltpu.VMEM((rows, width), F32),
                pltpu.VMEM((rows, width), F32),
                pltpu.VMEM((levels, heads) + square, F32),
                pltpu.VMEM((heads,) + square, F32),
                pltpu.VMEM((heads,) + square, F32),
                pltpu.VMEM((levels, heads) + square, BF16),
                pltpu.VMEM((levels, heads) + square, BF16),
                pltpu.VMEM((levels, heads) + square, BF16),
                pltpu.VMEM((levels, heads) + square, BF16),
                dma((4,)),
                dma((chips, 2)),
                dma,
                dma((chips, chunks)),
                dma((chips, chunks)),
                dma((chips, chunks)),
                dma((chips, chunks)),
                dma,
                dma,
                dma((levels,)),
                dma((levels,)),
                dma((levels, heads, PIECES)),
                dma((levels, heads, PIECES)),
            ],
            compiler_params=pltpu.CompilerParams(
                collective_id=0, has_side_effects=True, vmem_limit_bytes=32768 * 1024
            ),
        )(*[pltpu.with_memory_space_constraint(x, pltpu.HBM) for x in (queries, key_rows, value_rows, out_grad, out_weight, level_codes.T)])
        return pl.pallas_call(
            place,
            out_shape=(result,) * 3,
            in_specs=[pl.BlockSpec(memory_space=pltpu.VMEM)] * 3,
            out_specs=(pl.BlockSpec(memory_space=pl.ANY),) * 3,
            scratch_shapes=[dma((3,))],
            compiler_params=pltpu.CompilerParams(vmem_limit_bytes=8 * 1024 * 1024),
        )(*grads)

    sharded = P(("seqa", "seqb"), "tp")
    return jax.shard_map(
        per_device,
        mesh=mesh,
        in_specs=(sharded,) * 4 + (P("tp", None), sharded),
        out_specs=(sharded,) * 3,
        check_vma=False,
    )
```
